32 devices in a mesh: row: 8 (over y, x, core), col: 4 (over z).
Axes of the slice: x: 2, y: 2, z: 4, core: 2. Of those that a mesh axis runs over, the one named last changes fastest.
Arguments:
- database: bfloat16 [4096, 16384], P('row', 'col'), may hold values from -1 to 1
- query: bfloat16 [64, 4096], P('col', 'row'), may hold values from -8 to 8
- slot_map: int32 [64], replicated, may hold values from 0 to 63, each once
- keys: bfloat16 [64, 2048, 512], P(('row', 'col')), may hold values from -0.125 to 0.125
Outputs:
- packed: float32 [64, 8, 512], P(('row', 'col'))
The draws below stay inside these ranges and needn't reach their ends.
Inputs may be any that keep to these rules, and one draw needn't show every extreme that they name: `slot_map`: each slot serves a different client.
All inputs are finite; a program needn't handle non-finite values.
Results may differ from the reference program's by a relative error of at most 0.0085.
Values may be sent and summed in bfloat16 or wider, within the bound.
No kernel may reach another device: no remote copies, remote signals or barrier semaphores. Data moves between devices by JAX's collectives and lax.ppermute only.
A program may use at most 64 MiB of HBM per device.

```python
import jax
import jax.numpy as jnp
from jax import lax

TILE = 2048
PACK = 512
QUERIES = 64
DBROWS = 4096
DBCOLS = 16384


def draw_query(key, part):
    first = jax.random.fold_in(jax.random.fold_in(key, 11), 0)
    base = jax.random.normal(first, (QUERIES, DBROWS), jnp.float32)
    values = jnp.clip(base, -8.0, 8.0)
    return values.astype(jnp.bfloat16)


def shard_levels(own_key, shape, pieces, least, largest):
    gain = 1.0
    for dim, shards_of in pieces:
        steps = jax.random.uniform(jax.random.fold_in(jax.random.fold_in(own_key, 6), dim), (shards_of,), jnp.float32, least / len(pieces), largest / len(pieces))
        gain = gain * jnp.repeat(jnp.exp(steps), shape[dim] // shards_of).reshape((-1,) + (1,) * (len(shape) - 1 - dim))
    return gain


def normal_values(own_key, shape, spread, reach, cuts=(), dtype=jnp.bfloat16):
    array = spread * jax.random.normal(own_key, shape, jnp.float32)
    if cuts:
        array = array * shard_levels(own_key, shape, cuts, -0.22, 0.18)
    return jnp.clip(array, -reach, reach).astype(dtype)


def setup_inputs(seed: int = 0) -> dict:
    streams_of = jax.random.split(jax.random.key(seed), 5)
    database = jnp.clip(jax.random.uniform(streams_of[0], (DBROWS, DBCOLS), jnp.float32, -1.0, 1.0) * shard_levels(streams_of[0], (DBROWS, DBCOLS), ((0, 8), (1, 4)), -0.4, 0.0), -1.0, 1.0).astype(jnp.bfloat16)
    query = draw_query(jax.random.fold_in(streams_of[4], 71), 0)
    slot_map = jax.random.permutation(streams_of[2], QUERIES).astype(jnp.int32)
    keys = normal_values(streams_of[3], (QUERIES, TILE, PACK), TILE ** -0.5, 0.125, ((0, 32),))
    return dict(database=database, query=query, slot_map=slot_map, keys=keys)


def pack_slot(pair):
    tiles, block = pair
    return jnp.dot(tiles.astype(jnp.float32), block.astype(jnp.float32), preferred_element_type=jnp.float32)


def reference(database, query, slot_map, keys):
    chosen = jnp.take(query, slot_map, axis=0)
    answers = jnp.dot(chosen, database, preferred_element_type=jnp.float32)
    switched = (answers * (float(DBROWS) ** -0.5)).astype(jnp.bfloat16)
    tiles = switched.reshape(switched.shape[0], -1, TILE)
    return lax.map(pack_slot, (tiles, keys))
```

```python
import jax
import jax.numpy as jnp
from jax import lax
from jax.sharding import PartitionSpec as P


def shards(database, query, slot_map, keys):
    rows_axis = lax.axis_size("row")
    cols_axis = lax.axis_size("col")
    factor = float(database.shape[0] * rows_axis) ** (-0.5)
    gathered = lax.all_gather(query, "col", axis=0, tiled=True)
    total, width = gathered.shape[0], database.shape[1]
    owned_count = total // (rows_axis * cols_axis)
    chosen = jnp.take(gathered, slot_map, axis=0)
    partial_value = jnp.dot(chosen, database, preferred_element_type=jnp.float32)
    blocks = partial_value.astype(jnp.bfloat16).reshape(rows_axis, -1, width)
    parts = lax.all_to_all(blocks, "row", split_axis=0, concat_axis=0, tiled=True)
    answers = jnp.sum(parts.astype(jnp.float32), axis=0)
    switched = (answers * factor).astype(jnp.bfloat16)
    owned = lax.all_to_all(switched, "col", split_axis=0, concat_axis=1, tiled=True)
    tiles = owned.reshape(owned_count, -1, keys.shape[1])
    return jnp.einsum("ptj,pjk->ptk", tiles, keys, preferred_element_type=jnp.float32)


def solution(mesh):
    placed = (P("row", "col"), P("col", "row"), P(), P(("row", "col"), None, None))
    return jax.shard_map(
        shards, mesh=mesh, in_specs=placed, out_specs=P(("row", "col"), None, None), check_vma=False
    )
```

```python
import functools

import jax
import jax.numpy as jnp
from jax import lax
from jax.experimental import pallas as pl
from jax.experimental.pallas import tpu as pltpu
from jax.sharding import PartitionSpec as P


BF, F32 = jnp.bfloat16, jnp.float32
HBM = pl.BlockSpec(memory_space=pltpu.HBM)
VMEM = pl.BlockSpec(memory_space=pltpu.VMEM)
MIB = 1 << 20


def call(body, outs, ins, cost, scratch=(), limit=16 * MIB):
    return pl.pallas_call(
        body,
        out_shape=outs,
        in_specs=ins,
        out_specs=jax.tree.map(lambda _: VMEM, outs),
        scratch_shapes=list(scratch),
        compiler_params=pltpu.CompilerParams(vmem_limit_bytes=limit),
        cost_estimate=pl.CostEstimate(flops=cost[0], bytes_accessed=cost[1], transcendentals=0),
    )


def turn_order(rows):
    return sorted(range(1, rows // 2), key=lambda n: -n.bit_count())


def order_body(rows, cols, own, wanted_out, source_out):
    total = wanted_out.shape[0]
    each = total // (rows * cols)
    r, c = lax.axis_index("row"), lax.axis_index("col")
    i = lax.broadcasted_iota(jnp.int32, (total, total), 0)
    p = lax.broadcasted_iota(jnp.int32, (total, total), 1)
    group, rest = lax.div(i, cols * each), lax.rem(i, cols * each)
    step, lane = lax.div(rest, each), lax.rem(rest, each)
    half = rows // 2
    turn = jnp.where(group < half, 2 * group, 2 * (group - half) + 1)
    slot = ((turn ^ r) * cols + (step ^ c)) * each + lane
    wanted_out[...] = jnp.where(slot == p, 1.0, 0.0).astype(BF)
    source_out[...] = (c ^ lax.div(i, own)) * own + lax.rem(i, own)


def product_body(pieces, wanted, source, slots, *refs):
    queries, (database, keep, send) = refs[:pieces], refs[pieces:]
    served = jnp.where(slots[...] == source[...], 1.0, 0.0).astype(BF)
    pick = lax.dot_general(
        wanted[...], served, (((1,), (1,)), ((), ())), preferred_element_type=F32
    ).astype(BF)
    gathered = jnp.concatenate([q[...] for q in queries], axis=0)
    chosen = jnp.dot(pick, gathered, preferred_element_type=F32).astype(BF)
    half = keep.shape[0]
    value = jnp.dot(chosen, database[...], preferred_element_type=F32)
    keep[...] = value[:half]
    send[...] = value[half:].astype(BF)


def halve_body(keep, got, own, *sends):
    rows = own.shape[0]
    own[...] = keep[:rows] + got[:rows].astype(F32)
    for n, out in enumerate(sends, 1):
        part = slice(n * rows, (n + 1) * rows)
        out[...] = (keep[part] + got[part].astype(F32)).astype(BF)


def switch_body(factor, arrivals, own, *refs):
    got, outs = refs[:arrivals], refs[arrivals:]
    value = own[...]
    for ref in got:
        value = value + ref[...].astype(F32)
    switched = (value * factor).astype(F32)
    each = outs[0].shape[0]
    for n, out in enumerate(outs):
        out[...] = switched[n * each : (n + 1) * each].astype(BF)


def pack_body(cols, *refs):
    got, (keys, out, tiles) = refs[:cols], refs[cols:]
    count, depth = keys.shape[0], keys.shape[1]
    per = got[0].shape[1] // depth
    c = lax.axis_index("col")
    for s in range(count):
        for k in range(cols):
            source = c ^ k
            for h in range(per):
                row = got[k][s : s + 1, h * depth : (h + 1) * depth].astype(F32)
                tiles[s, pl.ds(source * per + h, 1), :] = row
        out[s] = jnp.dot(tiles[s].astype(BF), keys[s], preferred_element_type=F32)


def shards(database, query, slot_map, keys):
    rows, cols = lax.axis_size("row"), lax.axis_size("col")
    own, depth = query.shape
    width = database.shape[1]
    total = own * cols
    each = total // (rows * cols)
    half, block = total // 2, total // rows
    factor = float(depth * rows) ** (-0.5)
    S = jax.ShapeDtypeStruct

    def along_row(x, k):
        return lax.ppermute(x, "row", [(i, i ^ k) for i in range(rows)])

    def along_col(x, k):
        return lax.ppermute(x, "col", [(i, i ^ k) for i in range(cols)])

    hops = range(1, cols)
    arrived = dict((k, along_col(query, k)) for k in hops)
    wanted, source = call(
        functools.partial(order_body, rows, cols, own),
        (S((total, total), BF), S((total, total), jnp.int32)),
        [],
        (10**10, 10 * MIB),
    )()
    keep, send = call(
        functools.partial(product_body, cols),
        (S((half, width), F32), S((half, width), BF)),
        [VMEM] * (cols + 4),
        (2 * total * depth * width, database.size * 2),
    )(wanted, source, slot_map.reshape(1, total), query, *[arrived[k] for k in range(1, cols)], database)
    got = along_row(send, 1)
    kept, *sends = call(
        halve_body,
        [S((block, width), F32)] + [S((block, width), BF)] * (rows // 2 - 1),
        [VMEM, VMEM],
        (half * width, half * width * 6),
    )(keep, got)
    turns = turn_order(rows)
    swapped = [along_row(sends[n - 1], 2 * n) for n in turns]
    outs = call(
        functools.partial(switch_body, factor, rows // 2 - 1),
        [S((each, width), BF)] * cols,
        [VMEM] * (rows // 2),
        (block * width * rows, block * width * 8),
    )(kept, *swapped)
    moved = dict((k, along_col(outs[k], k)) for k in range(1, cols))
    blocks = [outs[0]] + [moved[k] for k in range(1, cols)]
    tiles = cols * width // keys.shape[1]
    return call(
        functools.partial(pack_body, cols),
        S((each, tiles, keys.shape[2]), F32),
        [VMEM] * (cols + 1),
        (2 * each * tiles * keys.shape[1] * keys.shape[2], keys.size * 2),
        [pltpu.VMEM((each, tiles, keys.shape[1]), F32)],
    )(*blocks, keys)


def solution(mesh):
    placed = (P("row", "col"), P("col", "row"), P(), P(("row", "col"), None, None))
    return jax.shard_map(
        shards, mesh=mesh, in_specs=placed, out_specs=P(("row", "col"), None, None), check_vma=False
    )
```

```python
import functools

import jax
import jax.numpy as jnp
from jax import lax
from jax.experimental import pallas as pl
from jax.experimental.pallas import tpu as pltpu
from jax.sharding import PartitionSpec as P


BF, F32 = jnp.bfloat16, jnp.float32
VMEM = pl.BlockSpec(memory_space=pltpu.VMEM)
MIB = 1 << 20
COVER = 10**10


def call(body, outs, operands, flops, nbytes, scratch=()):
    return pl.pallas_call(
        body,
        out_shape=outs,
        in_specs=[VMEM] * len(operands),
        out_specs=jax.tree.map(lambda _: VMEM, outs),
        scratch_shapes=list(scratch),
        compiler_params=pltpu.CompilerParams(vmem_limit_bytes=16 * MIB),
        cost_estimate=pl.CostEstimate(flops=flops, bytes_accessed=nbytes, transcendentals=0),
    )(*operands)


def lookup(table, index):
    out = jnp.full_like(index, table[0])
    for n, value in enumerate(table[1:], 1):
        out = jnp.where(index == n, value, out)
    return out


def ring_of(cols):
    return [i ^ (i >> 1) for i in range(cols)]


def turns_of(rows):
    return [2 * n for n in sorted(range(1, rows // 2), key=lambda n: -n.bit_count())] + [0]


def order_body(rows, cols, own, wanted, source):
    total = wanted.shape[0]
    each = total // (rows * cols)
    r, c = lax.axis_index("row"), lax.axis_index("col")
    i = lax.broadcasted_iota(jnp.int32, (total, total), 0)
    p = lax.broadcasted_iota(jnp.int32, (total, total), 1)
    group, rest = lax.div(i, cols * each), lax.rem(i, cols * each)
    step, lane = lax.div(rest, each), lax.rem(rest, each)
    turns = turns_of(rows)
    turn = lookup(turns + [t + 1 for t in turns], group)
    slot = ((turn ^ r) * cols + (step ^ c)) * each + lane
    wanted[...] = jnp.where(slot == p, 1.0, 0.0).astype(BF)
    ring = ring_of(cols)
    place = lookup([ring.index(n) for n in range(cols)], c + 0 * i)
    origin = lookup(ring, lax.rem(place - lax.div(i, own) + cols, cols))
    source[...] = origin * own + lax.rem(i, own)


def pick_body(wanted, source, slots, pick):
    served = jnp.where(slots[...] == source[...], 1.0, 0.0).astype(BF)
    pick[...] = lax.dot_general(
        wanted[...], served, (((1,), (1,)), ((), ())), preferred_element_type=F32
    ).astype(BF)


def product_body(pieces, pick, *refs):
    queries, (database, keep, first, rest) = refs[:pieces], refs[pieces:]
    gathered = jnp.concatenate([q[...] for q in queries], axis=0)
    chosen = jnp.dot(pick[...], gathered, preferred_element_type=F32).astype(BF)
    half, block = keep.shape[0], first.shape[0]
    value = jnp.dot(chosen, database[...], preferred_element_type=F32)
    keep[...] = value[:half]
    first[...] = value[half : half + block].astype(BF)
    rest[...] = value[half + block :].astype(BF)


def first_body(keep, got, out):
    out[...] = (keep[: out.shape[0]] + got[...].astype(F32)).astype(BF)


def rest_body(keep, got, *outs):
    rows = outs[0].shape[0]
    for n, out in enumerate(outs):
        value = keep[(n + 1) * rows : (n + 2) * rows] + got[n * rows : (n + 1) * rows].astype(F32)
        out[...] = value.astype(out.dtype)


def switch_body(factor, arrivals, own, *refs):
    got, outs = refs[:arrivals], refs[arrivals:]
    value = own[...]
    for ref in got:
        value = value + ref[...].astype(F32)
    switched = value * factor
    each = outs[0].shape[0]
    for n, out in enumerate(outs):
        out[...] = switched[n * each : (n + 1) * each].astype(BF)


def pack_body(cols, *refs):
    got, (keys, out, tiles) = refs[:cols], refs[cols:]
    count, depth = keys.shape[0], keys.shape[1]
    per = got[0].shape[1] // depth
    c = lax.axis_index("col")
    for s in range(count):
        for k in range(cols):
            for h in range(per):
                row = got[k][s : s + 1, h * depth : (h + 1) * depth].astype(F32)
                tiles[s, pl.ds((c ^ k) * per + h, 1), :] = row
        out[s] = jnp.dot(tiles[s].astype(BF), keys[s], preferred_element_type=F32)


def shards(database, query, slot_map, keys):
    rows, cols = lax.axis_size("row"), lax.axis_size("col")
    own, depth = query.shape
    width = database.shape[1]
    total = own * cols
    each = total // (rows * cols)
    half, block = total // 2, total // rows
    factor = float(depth * rows) ** (-0.5)
    S = jax.ShapeDtypeStruct
    ring, turns = ring_of(cols), turns_of(rows)

    def along_row(x, k):
        return lax.ppermute(x, "row", [(i, i ^ k) for i in range(rows)])

    arrived = [
        lax.ppermute(query, "col", [(ring[i], ring[(i + k) % cols]) for i in range(cols)])
        for k in range(1, cols)
    ]
    wanted, source = call(
        functools.partial(order_body, rows, cols, own),
        [S((total, total), BF), S((total, total), jnp.int32)],
        [],
        COVER,
        8 * total * total,
    )
    pick = call(
        pick_body,
        S((total, total), BF),
        [wanted, source, slot_map.reshape(1, total)],
        2 * total**3,
        8 * total * total,
    )
    keep, first, rest = call(
        functools.partial(product_body, cols),
        [S((half, width), F32), S((block, width), BF), S((half - block, width), BF)],
        [pick, query, *arrived, database],
        2 * total * depth * width,
        database.size * 2,
    )
    first = along_row(first, 1)
    rest = along_row(rest, 1)
    lead = call(first_body, S((block, width), BF), [keep, first], block * width, 8 * block * width)
    lead = along_row(lead, turns[0])
    *others, kept = call(
        rest_body,
        [S((block, width), BF)] * (rows // 2 - 2) + [S((block, width), F32)],
        [keep, rest],
        half * width,
        6 * half * width,
    )
    swapped = [lead] + [along_row(x, turns[n]) for n, x in enumerate(others, 1)]
    outs = call(
        functools.partial(switch_body, factor, len(swapped)),
        [S((each, width), BF)] * cols,
        [kept, *swapped],
        block * width * rows,
        8 * block * width,
    )
    blocks = [outs[0]] + [
        lax.ppermute(outs[k], "col", [(i, i ^ k) for i in range(cols)])
        for k in range(1, cols)
    ]
    tiles = cols * width // keys.shape[1]
    return call(
        functools.partial(pack_body, cols),
        S((each, tiles, keys.shape[2]), F32),
        [*blocks, keys],
        2 * each * tiles * keys.shape[1] * keys.shape[2],
        keys.size * 2,
        [pltpu.VMEM((each, tiles, keys.shape[1]), F32)],
    )


def solution(mesh):
    placed = (P("row", "col"), P("col", "row"), P(), P(("row", "col"), None, None))
    return jax.shard_map(
        shards, mesh=mesh, in_specs=placed, out_specs=P(("row", "col"), None, None), check_vma=False
    )
```

```python
import functools

import jax
import jax.numpy as jnp
from jax import lax
from jax.experimental import pallas as pl
from jax.experimental.pallas import tpu as pltpu
from jax.sharding import PartitionSpec as P


BF, F32 = jnp.bfloat16, jnp.float32
VMEM = pl.BlockSpec(memory_space=pltpu.VMEM)
MIB = 1 << 20
COVER = 10**10


def call(body, outs, operands, flops, nbytes, scratch=()):
    return pl.pallas_call(
        body,
        out_shape=outs,
        in_specs=[VMEM] * len(operands),
        out_specs=jax.tree.map(lambda _: VMEM, outs),
        scratch_shapes=list(scratch),
        compiler_params=pltpu.CompilerParams(vmem_limit_bytes=16 * MIB),
        cost_estimate=pl.CostEstimate(flops=flops, bytes_accessed=nbytes, transcendentals=0),
    )(*operands)


def lookup(table, index):
    out = jnp.full_like(index, table[0])
    for n, value in enumerate(table[1:], 1):
        out = jnp.where(index == n, value, out)
    return out


def ring_of(cols):
    return [i ^ (i >> 1) for i in range(cols)]


def turns_of(rows):
    return [2 * n + 1 for n in sorted(range(1, rows // 2), key=lambda n: -n.bit_count())] + [0]


def order_body(rows, cols, own, wanted, source):
    total = wanted.shape[0]
    each = total // (rows * cols)
    r, c = lax.axis_index("row"), lax.axis_index("col")
    i = lax.broadcasted_iota(jnp.int32, (total, total), 0)
    p = lax.broadcasted_iota(jnp.int32, (total, total), 1)
    group, rest = lax.div(i, cols * each), lax.rem(i, cols * each)
    step, lane = lax.div(rest, each), lax.rem(rest, each)
    turns = turns_of(rows)
    turn = lookup(turns + [t ^ 1 for t in turns], group)
    row = turn ^ r ^ jnp.where(step == 0, 0, 1)
    slot = (row * cols + (step ^ c)) * each + lane
    wanted[...] = jnp.where(slot == p, 1.0, 0.0).astype(BF)
    ring = ring_of(cols)
    place = lookup([ring.index(n) for n in range(cols)], c + 0 * i)
    origin = lookup(ring, lax.rem(place - lax.div(i, own) + cols, cols))
    source[...] = origin * own + lax.rem(i, own)


def pick_body(wanted, source, slots, pick):
    served = jnp.where(slots[...] == source[...], 1.0, 0.0).astype(BF)
    pick[...] = lax.dot_general(
        wanted[...], served, (((1,), (1,)), ((), ())), preferred_element_type=F32
    ).astype(BF)


def product_body(pieces, pick, *refs):
    queries, (database, keep, first, rest) = refs[:pieces], refs[pieces:]
    gathered = jnp.concatenate([q[...] for q in queries], axis=0)
    chosen = jnp.dot(pick[...], gathered, preferred_element_type=F32).astype(BF)
    half, block = keep.shape[0], first.shape[0]
    value = jnp.dot(chosen, database[...], preferred_element_type=F32)
    keep[...] = value[:half]
    first[...] = value[half : half + block].astype(BF)
    rest[...] = value[half + block :].astype(BF)


def first_body(keep, got, out):
    out[...] = (keep[: out.shape[0]] + got[...].astype(F32)).astype(BF)


def rest_body(keep, got, *outs):
    rows = outs[0].shape[0]
    for n, out in enumerate(outs):
        value = keep[(n + 1) * rows : (n + 2) * rows] + got[n * rows : (n + 1) * rows].astype(F32)
        out[...] = value.astype(out.dtype)


def switch_body(factor, arrivals, own, *refs):
    got, outs = refs[:arrivals], refs[arrivals:]
    value = own[...]
    for ref in got:
        value = value + ref[...].astype(F32)
    switched = value * factor
    each = outs[0].shape[0]
    for n, out in enumerate(outs):
        out[...] = switched[n * each : (n + 1) * each].astype(BF)


def pack_body(cols, *refs):
    got, (keys, out, tiles) = refs[:cols], refs[cols:]
    count, depth = keys.shape[0], keys.shape[1]
    per = got[0].shape[1] // depth
    c = lax.axis_index("col")
    for s in range(count):
        for k in range(cols):
            for h in range(per):
                row = got[k][s : s + 1, h * depth : (h + 1) * depth].astype(F32)
                tiles[s, pl.ds((c ^ k) * per + h, 1), :] = row
        out[s] = jnp.dot(tiles[s].astype(BF), keys[s], preferred_element_type=F32)


def shards(database, query, slot_map, keys):
    rows, cols = lax.axis_size("row"), lax.axis_size("col")
    own, depth = query.shape
    width = database.shape[1]
    total = own * cols
    each = total // (rows * cols)
    half, block = total // 2, total // rows
    factor = float(depth * rows) ** (-0.5)
    S = jax.ShapeDtypeStruct
    ring, turns = ring_of(cols), turns_of(rows)

    def along_row(x, k):
        return lax.ppermute(x, "row", [(i, i ^ k) for i in range(rows)])

    arrived = [
        lax.ppermute(query, "col", [(ring[i], ring[(i + k) % cols]) for i in range(cols)])
        for k in range(1, cols)
    ]
    wanted, source = call(
        functools.partial(order_body, rows, cols, own),
        [S((total, total), BF), S((total, total), jnp.int32)],
        [],
        COVER,
        8 * total * total,
    )
    pick = call(
        pick_body,
        S((total, total), BF),
        [wanted, source, slot_map.reshape(1, total)],
        2 * total**3,
        8 * total * total,
    )
    keep, first, rest = call(
        functools.partial(product_body, cols),
        [S((half, width), F32), S((block, width), BF), S((half - block, width), BF)],
        [pick, query, *arrived, database],
        2 * total * depth * width,
        database.size * 2,
    )
    first = along_row(first, 1)
    rest = along_row(rest, 1)
    lead = call(first_body, S((block, width), BF), [keep, first], block * width, 8 * block * width)
    lead = along_row(lead, turns[0])
    *others, kept = call(
        rest_body,
        [S((block, width), BF)] * (rows // 2 - 2) + [S((block, width), F32)],
        [keep, rest],
        half * width,
        6 * half * width,
    )
    swapped = [lead] + [along_row(x, turns[n]) for n, x in enumerate(others, 1)]
    outs = call(
        functools.partial(switch_body, factor, len(swapped)),
        [S((each, width), BF)] * cols,
        [kept, *swapped],
        block * width * rows,
        8 * block * width,
    )
    blocks = [outs[0]] + [
        lax.ppermute(outs[k], ("row", "col"), [(i, i ^ (cols + k)) for i in range(rows * cols)])
        for k in range(1, cols)
    ]
    tiles = cols * width // keys.shape[1]
    return call(
        functools.partial(pack_body, cols),
        S((each, tiles, keys.shape[2]), F32),
        [*blocks, keys],
        2 * each * tiles * keys.shape[1] * keys.shape[2],
        keys.size * 2,
        [pltpu.VMEM((each, tiles, keys.shape[1]), F32)],
    )


def solution(mesh):
    placed = (P("row", "col"), P("col", "row"), P(), P(("row", "col"), None, None))
    return jax.shard_map(
        shards, mesh=mesh, in_specs=placed, out_specs=P(("row", "col"), None, None), check_vma=False
    )
```

```python
import functools

import jax
import jax.numpy as jnp
from jax import lax
from jax.experimental import pallas as pl
from jax.experimental.pallas import tpu as pltpu
from jax.sharding import PartitionSpec as P


BF, F32 = jnp.bfloat16, jnp.float32
VMEM = pl.BlockSpec(memory_space=pltpu.VMEM)
MIB = 1 << 20
COVER = 10**10


def call(body, outs, operands, flops, nbytes, scratch=()):
    return pl.pallas_call(
        body,
        out_shape=outs,
        in_specs=[VMEM] * len(operands),
        out_specs=jax.tree.map(lambda _: VMEM, outs),
        scratch_shapes=list(scratch),
        compiler_params=pltpu.CompilerParams(vmem_limit_bytes=16 * MIB),
        cost_estimate=pl.CostEstimate(flops=flops, bytes_accessed=nbytes, transcendentals=0),
    )(*operands)


def lookup(table, index):
    out = jnp.full_like(index, table[0])
    for n, value in enumerate(table[1:], 1):
        out = jnp.where(index == n, value, out)
    return out


def ring_of(cols):
    return [i ^ (i >> 1) for i in range(cols)]


def turns_of(rows):
    return [2 * n + 1 for n in range(rows // 2 - 1, 0, -1)] + [0]


def order_body(rows, cols, own, wanted, source):
    total = wanted.shape[0]
    each = total // (rows * cols)
    r, c = lax.axis_index("row"), lax.axis_index("col")
    i = lax.broadcasted_iota(jnp.int32, (total, total), 0)
    p = lax.broadcasted_iota(jnp.int32, (total, total), 1)
    group, rest = lax.div(i, cols * each), lax.rem(i, cols * each)
    step, lane = lax.div(rest, each), lax.rem(rest, each)
    turns = turns_of(rows)
    away = [t ^ 1 for t in turns]
    turn = lookup(turns[:1] + away[:1] + turns[1:] + away[1:], group)
    row = turn ^ r ^ jnp.where(step == 0, 0, 1)
    slot = (row * cols + (step ^ c)) * each + lane
    wanted[...] = jnp.where(slot == p, 1.0, 0.0).astype(BF)
    ring = ring_of(cols)
    place = lookup([ring.index(n) for n in range(cols)], c + 0 * i)
    origin = lookup(ring, lax.rem(place - lax.div(i, own) + cols, cols))
    source[...] = origin * own + lax.rem(i, own)


def pick_body(wanted, source, slots, pick):
    served = jnp.where(slots[...] == source[...], 1.0, 0.0).astype(BF)
    pick[...] = lax.dot_general(
        wanted[...], served, (((1,), (1,)), ((), ())), preferred_element_type=F32
    ).astype(BF)


def lead_body(pieces, pick, *refs):
    queries, (database, chosen, keep, away) = refs[:pieces], refs[pieces:]
    gathered = jnp.concatenate([q[...] for q in queries], axis=0)
    rows = jnp.dot(pick[...], gathered, preferred_element_type=F32).astype(BF)
    block = keep.shape[0]
    chosen[...] = rows[2 * block :]
    value = jnp.dot(rows[: 2 * block], database[...], preferred_element_type=F32)
    keep[...] = value[:block]
    away[...] = value[block:].astype(BF)


def bulk_body(chosen, database, keep, away):
    value = jnp.dot(chosen[...], database[...], preferred_element_type=F32)
    half = keep.shape[0]
    keep[...] = value[:half]
    away[...] = value[half:].astype(BF)


def first_body(keep, got, out):
    out[...] = (keep[...] + got[...].astype(F32)).astype(BF)


def rest_body(keep, got, *outs):
    rows = outs[0].shape[0]
    for n, out in enumerate(outs):
        value = keep[n * rows : (n + 1) * rows] + got[n * rows : (n + 1) * rows].astype(F32)
        out[...] = value.astype(out.dtype)


def switch_body(factor, arrivals, own, *refs):
    got, outs = refs[:arrivals], refs[arrivals:]
    value = own[...]
    for ref in got:
        value = value + ref[...].astype(F32)
    switched = value * factor
    each = outs[0].shape[0]
    for n, out in enumerate(outs):
        out[...] = switched[n * each : (n + 1) * each].astype(BF)


def pack_body(cols, *refs):
    got, (keys, out, tiles) = refs[:cols], refs[cols:]
    count, depth = keys.shape[0], keys.shape[1]
    per = got[0].shape[1] // depth
    c = lax.axis_index("col")
    for s in range(count):
        for k in range(cols):
            for h in range(per):
                row = got[k][s : s + 1, h * depth : (h + 1) * depth].astype(F32)
                tiles[s, pl.ds((c ^ k) * per + h, 1), :] = row
        out[s] = jnp.dot(tiles[s].astype(BF), keys[s], preferred_element_type=F32)


def shards(database, query, slot_map, keys):
    rows, cols = lax.axis_size("row"), lax.axis_size("col")
    own, depth = query.shape
    width = database.shape[1]
    total = own * cols
    each = total // (rows * cols)
    half, block = total // 2, total // rows
    factor = float(depth * rows) ** (-0.5)
    S = jax.ShapeDtypeStruct
    ring, turns = ring_of(cols), turns_of(rows)

    def along_row(x, k):
        return lax.ppermute(x, "row", [(i, i ^ k) for i in range(rows)])

    arrived = [
        lax.ppermute(query, "col", [(ring[i], ring[(i + k) % cols]) for i in range(cols)])
        for k in range(1, cols)
    ]
    wanted, source = call(
        functools.partial(order_body, rows, cols, own),
        [S((total, total), BF), S((total, total), jnp.int32)],
        [],
        COVER,
        8 * total * total,
    )
    pick = call(
        pick_body,
        S((total, total), BF),
        [wanted, source, slot_map.reshape(1, total)],
        2 * total**3,
        8 * total * total,
    )
    chosen, kept_first, first = call(
        functools.partial(lead_body, cols),
        [S((total - 2 * block, depth), BF), S((block, width), F32), S((block, width), BF)],
        [pick, query, *arrived, database],
        4 * block * depth * width,
        database.size * 2,
    )
    first = along_row(first, 1)
    bulk = half - block
    kept_rest, rest = call(
        bulk_body,
        [S((bulk, width), F32), S((bulk, width), BF)],
        [chosen, database],
        4 * bulk * depth * width,
        database.size * 2,
    )
    rest = along_row(rest, 1)
    lead = call(first_body, S((block, width), BF), [kept_first, first], block * width, 8 * block * width)
    lead = along_row(lead, turns[0])
    *others, kept = call(
        rest_body,
        [S((block, width), BF)] * (rows // 2 - 2) + [S((block, width), F32)],
        [kept_rest, rest],
        half * width,
        6 * half * width,
    )
    swapped = [lead] + [along_row(x, turns[n]) for n, x in enumerate(others, 1)]
    outs = call(
        functools.partial(switch_body, factor, len(swapped)),
        [S((each, width), BF)] * cols,
        [kept, *swapped],
        block * width * rows,
        8 * block * width,
    )
    blocks = [outs[0]] + [
        lax.ppermute(outs[k], ("row", "col"), [(i, i ^ (cols + k)) for i in range(rows * cols)])
        for k in range(1, cols)
    ]
    tiles = cols * width // keys.shape[1]
    return call(
        functools.partial(pack_body, cols),
        S((each, tiles, keys.shape[2]), F32),
        [*blocks, keys],
        2 * each * tiles * keys.shape[1] * keys.shape[2],
        keys.size * 2,
        [pltpu.VMEM((each, tiles, keys.shape[1]), F32)],
    )


def solution(mesh):
    placed = (P("row", "col"), P("col", "row"), P(), P(("row", "col"), None, None))
    return jax.shard_map(
        shards, mesh=mesh, in_specs=placed, out_specs=P(("row", "col"), None, None), check_vma=False
    )
```

```python
import functools

import jax
import jax.numpy as jnp
from jax import lax
from jax.experimental import pallas as pl
from jax.experimental.pallas import tpu as pltpu
from jax.sharding import PartitionSpec as P


BF, F32 = jnp.bfloat16, jnp.float32
VMEM = pl.BlockSpec(memory_space=pltpu.VMEM)
MIB = 1 << 20
COVER = 10**10


def call(body, outs, operands, flops, nbytes, scratch=()):
    return pl.pallas_call(
        body,
        out_shape=outs,
        in_specs=[VMEM] * len(operands),
        out_specs=jax.tree.map(lambda _: VMEM, outs),
        scratch_shapes=list(scratch),
        compiler_params=pltpu.CompilerParams(vmem_limit_bytes=16 * MIB),
        cost_estimate=pl.CostEstimate(flops=flops, bytes_accessed=nbytes, transcendentals=0),
    )(*operands)


def lookup(table, index):
    out = jnp.full_like(index, table[0])
    for n, value in enumerate(table[1:], 1):
        out = jnp.where(index == n, value, out)
    return out


def ring_of(cols):
    return [i ^ (i >> 1) for i in range(cols)]


def turns_of(rows):
    return [2 * n + 1 for n in range(rows // 2 - 1, 0, -1)] + [0]


def order_body(rows, cols, own, wanted, source):
    total = wanted.shape[0]
    each = total // (rows * cols)
    r, c = lax.axis_index("row"), lax.axis_index("col")
    i = lax.broadcasted_iota(jnp.int32, (total, total), 0)
    p = lax.broadcasted_iota(jnp.int32, (total, total), 1)
    group, rest = lax.div(i, cols * each), lax.rem(i, cols * each)
    step, lane = lax.div(rest, each), lax.rem(rest, each)
    turns = turns_of(rows)
    turn = lookup(turns + [t ^ 1 for t in turns], group)
    row = turn ^ r ^ jnp.where(step == 0, 0, 1)
    slot = (row * cols + (step ^ c)) * each + lane
    wanted[...] = jnp.where(slot == p, 1.0, 0.0).astype(BF)
    ring = ring_of(cols)
    place = lookup([ring.index(n) for n in range(cols)], c + 0 * i)
    hop = lax.div(i, own)
    hop = jnp.where(lax.rem(r + 0 * i, 2) == 0, hop, lax.rem(cols - hop, cols))
    origin = lookup(ring, lax.rem(place - hop + cols, cols))
    source[...] = origin * own + lax.rem(i, own)


def pick_body(wanted, source, slots, pick):
    served = jnp.where(slots[...] == source[...], 1.0, 0.0).astype(BF)
    pick[...] = lax.dot_general(
        wanted[...], served, (((1,), (1,)), ((), ())), preferred_element_type=F32
    ).astype(BF)


def product_body(pieces, pick, *refs):
    queries, (database, keep, first, rest) = refs[:pieces], refs[pieces:]
    gathered = jnp.concatenate([q[...] for q in queries], axis=0)
    chosen = jnp.dot(pick[...], gathered, preferred_element_type=F32).astype(BF)
    half, block = keep.shape[0], first.shape[0]
    value = jnp.dot(chosen, database[...], preferred_element_type=F32)
    keep[...] = value[:half]
    first[...] = value[half : half + block].astype(BF)
    rest[...] = value[half + block :].astype(BF)


def first_body(keep, got, out):
    out[...] = (keep[: out.shape[0]] + got[...].astype(F32)).astype(BF)


def rest_body(keep, got, *outs):
    rows = outs[0].shape[0]
    for n, out in enumerate(outs):
        value = keep[(n + 1) * rows : (n + 2) * rows] + got[n * rows : (n + 1) * rows].astype(F32)
        out[...] = value.astype(out.dtype)


def switch_body(factor, arrivals, own, *refs):
    got, outs = refs[:arrivals], refs[arrivals:]
    value = own[...]
    for ref in got:
        value = value + ref[...].astype(F32)
    switched = value * factor
    each = outs[0].shape[0]
    for n, out in enumerate(outs):
        out[...] = switched[n * each : (n + 1) * each].astype(BF)


def pack_body(cols, *refs):
    got, (keys, out, tiles) = refs[:cols], refs[cols:]
    count, depth = keys.shape[0], keys.shape[1]
    per = got[0].shape[1] // depth
    c = lax.axis_index("col")
    for s in range(count):
        for k in range(cols):
            for h in range(per):
                row = got[k][s : s + 1, h * depth : (h + 1) * depth].astype(F32)
                tiles[s, pl.ds((c ^ k) * per + h, 1), :] = row
        out[s] = jnp.dot(tiles[s].astype(BF), keys[s], preferred_element_type=F32)


def shards(database, query, slot_map, keys):
    rows, cols = lax.axis_size("row"), lax.axis_size("col")
    own, depth = query.shape
    width = database.shape[1]
    total = own * cols
    each = total // (rows * cols)
    half, block = total // 2, total // rows
    factor = float(depth * rows) ** (-0.5)
    S = jax.ShapeDtypeStruct
    ring, turns = ring_of(cols), turns_of(rows)

    def along_row(x, k):
        return lax.ppermute(x, "row", [(i, i ^ k) for i in range(rows)])

    arrived = [
        lax.ppermute(
            query,
            ("row", "col"),
            [
                (r * cols + ring[i], r * cols + ring[(i + (cols - k if r % 2 else k)) % cols])
                for r in range(rows)
                for i in range(cols)
            ],
        )
        for k in range(1, cols)
    ]
    wanted, source = call(
        functools.partial(order_body, rows, cols, own),
        [S((total, total), BF), S((total, total), jnp.int32)],
        [],
        COVER,
        8 * total * total,
    )
    pick = call(
        pick_body,
        S((total, total), BF),
        [wanted, source, slot_map.reshape(1, total)],
        2 * total**3,
        8 * total * total,
    )
    keep, first, rest = call(
        functools.partial(product_body, cols),
        [S((half, width), F32), S((block, width), BF), S((half - block, width), BF)],
        [pick, query, *arrived, database],
        2 * total * depth * width,
        database.size * 2,
    )
    first = along_row(first, 1)
    rest = along_row(rest, 1)
    lead = call(first_body, S((block, width), BF), [keep, first], block * width, 8 * block * width)
    lead = along_row(lead, turns[0])
    *others, kept = call(
        rest_body,
        [S((block, width), BF)] * (rows // 2 - 2) + [S((block, width), F32)],
        [keep, rest],
        half * width,
        6 * half * width,
    )
    swapped = [lead] + [along_row(x, turns[n]) for n, x in enumerate(others, 1)]
    outs = call(
        functools.partial(switch_body, factor, len(swapped)),
        [S((each, width), BF)] * cols,
        [kept, *swapped],
        block * width * rows,
        8 * block * width,
    )
    blocks = [outs[0]] + [
        lax.ppermute(outs[k], ("row", "col"), [(i, i ^ (cols + k)) for i in range(rows * cols)])
        for k in range(1, cols)
    ]
    tiles = cols * width // keys.shape[1]
    return call(
        functools.partial(pack_body, cols),
        S((each, tiles, keys.shape[2]), F32),
        [*blocks, keys],
        2 * each * tiles * keys.shape[1] * keys.shape[2],
        keys.size * 2,
        [pltpu.VMEM((each, tiles, keys.shape[1]), F32)],
    )


def solution(mesh):
    placed = (P("row", "col"), P("col", "row"), P(), P(("row", "col"), None, None))
    return jax.shard_map(
        shards, mesh=mesh, in_specs=placed, out_specs=P(("row", "col"), None, None), check_vma=False
    )
```
